256 devices in a mesh: seq: 32 (over x, y, core), head: 8 (over z).
Axes of the slice: x: 4, y: 4, z: 8, core: 2. Of those that a mesh axis runs over, the one named last changes fastest.
Arguments:
- queries: bfloat16 [32768, 64, 128], P(('seq', 'head')), may hold values from -8 to 8
- keys: bfloat16 [32768, 8, 128], P(('seq', 'head')), may hold values from -8 to 8
- values: bfloat16 [32768, 8, 128], P(('seq', 'head')), may hold values from -6 to 6
- ancestors: int32 [256, 8], P('seq'), may hold values from 0 to 255, as said below
- lengths: int32 [256], replicated, may hold values from 2 to 128
Outputs:
- attended: bfloat16 [32768, 64, 128], P(('seq', 'head'))
The draws below stay inside these ranges and needn't reach their ends.
Inputs may be any that keep to these rules, and one draw needn't show every extreme that they name: The 8 ancestors of a block are distinct blocks held on other indices of seq; the blocks of one index of seq name, all together, exactly 2 distinct blocks of each of 6 other indices and no other block.
All inputs are finite; a program needn't handle non-finite values.
Results may differ from the reference program's by a relative error of at most 0.0049.
Values may be sent and summed in bfloat16 or wider, within the bound.
No kernel may reach another device: no remote copies, remote signals or barrier semaphores. Data moves between devices by JAX's collectives and lax.ppermute only.
A program may use at most 64 MiB of HBM per device.

```python
import math
import jax
import jax.numpy as jnp
from jax import lax

H = 64
KVH = 8
HD = 128
BS = 128
MAXANC = 8
NOWN = 6
CAP = 2
BLK_DEV = 8
TOKENS = 32768


def draw_pair(key):
    base_key = jax.random.fold_in(key, 7)
    key_field = jnp.clip(jax.random.normal(jax.random.fold_in(base_key, 1), (TOKENS, KVH, HD), jnp.float32), -6.0, 6.0)
    query_field = jnp.clip(jax.random.normal(jax.random.fold_in(base_key, 2), (TOKENS, H, HD), jnp.float32), -6.0, 6.0)
    return (query_field, key_field)


def draw_queries(key, part):
    return draw_pair(key)[0].astype(jnp.bfloat16)


def draw_keys(key, part):
    return draw_pair(key)[1].astype(jnp.bfloat16)


def draw_ancestors(key, part):
    base_key = jax.random.fold_in(key, 21)
    device_count = TOKENS // (BLK_DEV * BS)
    pool_size = CAP * NOWN

    def per_device(device_key, device_id):
        shuffled = jax.random.permutation(jax.random.fold_in(device_key, 1), device_count - 1)[:NOWN]
        owners = shuffled + (shuffled >= device_id).astype(jnp.int32)
        owner_keys = jax.random.split(jax.random.fold_in(device_key, 2), NOWN)
        locals_picked = jax.vmap(lambda owner_key: jax.random.permutation(owner_key, BLK_DEV)[:CAP])(owner_keys)
        pool_ids = (owners[:, None] * BLK_DEV + locals_picked).reshape(pool_size)
        starts = jax.random.randint(jax.random.fold_in(device_key, 3), (BLK_DEV,), 0, pool_size)
        starts = starts.at[0].set(0).at[1].set(MAXANC)
        position = (starts[:, None] + jnp.arange(MAXANC)[None, :]) % pool_size
        return pool_ids[position]
    device_keys = jax.random.split(base_key, device_count)
    table = jax.vmap(per_device)(device_keys, jnp.arange(device_count, dtype=jnp.int32))
    return table.reshape(device_count * BLK_DEV, MAXANC).astype(jnp.int32)


def with_ends(entries, key, low, high):
    longest = entries.shape.index(max(entries.shape))
    spots = []
    for shift in (0, 1):
        where = [jax.random.randint(jax.random.fold_in(key, axis), (), 0, length) for axis, length in enumerate(entries.shape)]
        where[longest] = (where[longest] + shift) % entries.shape[longest]
        spots.append(tuple(where))
    return entries.at[spots[0]].set(low).at[spots[1]].set(high)


def levels(own_key, extent, cuts, smallest, high):
    loudness, own = 1.0, jax.random.fold_in(own_key, 6)
    for axis_at, blocks in cuts:
        steps = jnp.exp(jax.random.uniform(jax.random.fold_in(own, axis_at), (blocks,), jnp.float32, smallest / len(cuts), high / len(cuts)))
        loudness = loudness * jnp.repeat(steps, extent[axis_at] // blocks).reshape([-1 if axis == axis_at else 1 for axis in range(len(extent))])
    return loudness


def normal_values(rng, extent, deviation, most, cuts=(), held_as=jnp.bfloat16):
    drawn = deviation * jax.random.normal(rng, extent, jnp.float32)
    if cuts:
        drawn = drawn * levels(rng, extent, cuts, -0.22, 0.18)
    return jnp.clip(drawn, -most, most).astype(held_as)


def setup_inputs(seed: int = 0) -> dict:
    seeds = jax.random.split(jax.random.key(seed), 6)
    return {
        "queries": draw_queries(jax.random.fold_in(seeds[5], 71), 0),
        "keys": draw_keys(jax.random.fold_in(seeds[5], 71), 0),
        "values": normal_values(seeds[2], (TOKENS, KVH, HD), 1.0, 6.0, ((0, 256),)),
        "ancestors": draw_ancestors(jax.random.fold_in(seeds[5], 71), 0),
        "lengths": with_ends(jax.random.randint(seeds[4], (TOKENS // BS,), 2, BS + 1), jax.random.fold_in(seeds[4], 1), 2, BS).astype(jnp.int32),
    }


negative_fill = -1e+30

def attend_block(query_block, key_self, value_self, key_far, value_far, length_self, length_far):
    width = query_block.shape[-1]
    block_rows = key_self.shape[0]
    kv_groups = key_self.shape[1]
    far_count = key_far.shape[0]
    key_all = jnp.concatenate([key_self[None], key_far], axis=0).reshape(-1, kv_groups, width)
    value_all = jnp.concatenate([value_self[None], value_far], axis=0).reshape(-1, kv_groups, width)
    scores = jnp.einsum('tgsd,kgd->gstk', query_block.astype(jnp.float32), key_all.astype(jnp.float32))
    scores = scores * (1.0 / math.sqrt(width))
    offsets_row = jnp.arange(block_rows, dtype=jnp.int32)
    self_mask = (offsets_row[None, :] <= offsets_row[:, None]) & (offsets_row[None, :] < length_self)
    far_mask = (offsets_row[None, :] < length_far[:, None]).reshape(1, far_count * block_rows)
    far_mask = jnp.broadcast_to(far_mask, (block_rows, far_count * block_rows))
    allowed = jnp.concatenate([self_mask, far_mask], axis=1)
    scores = jnp.where(allowed, scores, negative_fill)
    largest = lax.optimization_barrier(jnp.max(scores, axis=-1, keepdims=True))
    exponent = jnp.exp(scores - largest)
    weights = (exponent / lax.optimization_barrier(jnp.sum(exponent, axis=-1, keepdims=True))).astype(jnp.bfloat16)
    mixed = jnp.einsum('gstk,kgd->tgsd', weights.astype(jnp.float32), value_all.astype(jnp.float32))
    return mixed.astype(jnp.bfloat16)

def reference(queries, keys, values, ancestors, lengths):
    block_count = TOKENS // BS
    query_grid = queries.reshape(block_count, BS, KVH, H // KVH, HD)
    key_grid = keys.reshape(block_count, BS, KVH, HD)
    value_grid = values.reshape(block_count, BS, KVH, HD)

    def one_block(block_id):
        chosen = ancestors[block_id]
        return attend_block(query_grid[block_id], key_grid[block_id], value_grid[block_id], jnp.take(key_grid, chosen, axis=0), jnp.take(value_grid, chosen, axis=0), lengths[block_id], jnp.take(lengths, chosen, axis=0))
    mixed = lax.map(one_block, jnp.arange(block_count, dtype=jnp.int32))
    return mixed.reshape(TOKENS, H, HD)
```

```python
import functools
import math

import jax
import jax.numpy as jnp
from jax import lax
from jax.experimental import pallas as pl
from jax.experimental.pallas import tpu as pltpu
from jax.sharding import PartitionSpec as P

BS = 128
POOL = 12
HALF = POOL // 2
TILE = 8
NEG = -1e30


def pool_of(ancestors):
    flat = ancestors.reshape(-1)
    n = flat.shape[0]
    order = jnp.arange(n, dtype=jnp.int32)
    same = flat[:, None] == flat[None, :]
    repeat = jnp.any(same & (order[None, :] < order[:, None]), axis=1)
    first = ~repeat
    rank = jnp.sum((first[None, :] & (flat[None, :] < flat[:, None])).astype(jnp.int32), axis=1)
    slots = jnp.arange(BS, dtype=jnp.int32)
    hit = first[:, None] & (rank[:, None] == slots[None, :])
    pool = jnp.sum(jnp.where(hit, flat[:, None], 0), axis=0)
    return pool, rank.reshape(ancestors.shape)


def pick_kernel(pools, held, low, high):
    def one(s, carry):
        for i in range(HALF):
            low[s, i] = held[pools[s, i]]
            high[s, i] = held[pools[s, HALF + i]]
        return carry

    lax.fori_loop(0, pools.shape[0], one, 0)


def pick(pools, held):
    groups = pools.shape[0]
    part = jax.ShapeDtypeStruct((groups, HALF, TILE, BS), held.dtype)
    whole = pl.BlockSpec(memory_space=pltpu.VMEM)
    return pl.pallas_call(
        pick_kernel,
        out_shape=(part, part),
        grid_spec=pltpu.PrefetchScalarGridSpec(
            num_scalar_prefetch=1, grid=(1,),
            in_specs=[pl.BlockSpec(held.shape, lambda i, _: (0, 0, 0))],
            out_specs=[pl.BlockSpec(part.shape, lambda i, _: (0, 0, 0, 0))] * 2,
        ),
        name="pick",
    )(pools, held)


def attend_kernel(scale, meta, q, own, low, high, _, out, keys, vals, acc):
    far = 8
    row = lax.broadcasted_iota(jnp.int32, (BS, BS), 0)

    def put(j, k, v, length):
        k = k.astype(jnp.float32).reshape(BS, BS)
        v = v.astype(jnp.float32).reshape(BS, BS)
        valid = row < length
        at = slice(j * BS, (j + 1) * BS)
        keys[at, :] = jnp.where(valid, k, k[0:1, :]).astype(jnp.bfloat16)
        vals[at, 0:BS] = jnp.where(valid, v, 0.0).astype(jnp.bfloat16)
        vals[at, BS:] = jnp.where(valid, 1.0, 0.0).astype(jnp.bfloat16)

    put(0, own[0:16, 0], own[16:32, 0], meta[17])
    for j in range(far):
        place, length = meta[1 + j], meta[9 + j]

        @pl.when(place < HALF)
        def _():
            put(j + 1, low[0:16, place], low[16:32, place], length)

        @pl.when(place >= HALF)
        def _():
            put(j + 1, high[0:16, place - HALF], high[16:32, place - HALF], length)

    tokens = 32
    rows = tokens * 8
    token = lax.broadcasted_iota(jnp.int32, (rows, BS), 0) // 8
    offset = lax.broadcasted_iota(jnp.int32, (rows, BS), 1)
    for i in range(BS // tokens):
        at = slice(i * tokens, (i + 1) * tokens)
        qt = q[at].astype(jnp.float32).reshape(rows, BS).astype(jnp.bfloat16)
        s = lax.dot_general(qt, keys[...], (((1,), (1,)), ((), ())), preferred_element_type=jnp.float32)
        s_own = jnp.where(offset <= token + i * tokens, s[:, 0:BS], NEG)
        s_far = s[:, BS:]
        m = jnp.maximum(jnp.max(s_own, axis=1, keepdims=True), jnp.max(s_far, axis=1, keepdims=True))
        p_own = jnp.exp2((s_own - m) * scale).astype(jnp.bfloat16)
        p_far = jnp.exp2((s_far - m) * scale).astype(jnp.bfloat16)
        o = jnp.dot(p_own, vals[0:BS, :], preferred_element_type=jnp.float32)
        o = o + jnp.dot(p_far, vals[BS:, :], preferred_element_type=jnp.float32)
        r = o[:, 0:BS] / o[:, BS:]
        out[at] = r.reshape(tokens, 8, BS).astype(out.dtype)


def attend(meta, q, own, low, high, prev):
    scale = math.log2(math.e) / math.sqrt(BS)
    shape = jax.ShapeDtypeStruct(q.shape, q.dtype)
    body = functools.partial(attend_kernel, scale)
    part = pl.BlockSpec(low.shape, lambda i, m: (0, 0, 0, 0))
    heads = pl.BlockSpec((BS, 8, BS), lambda i, m: (0, m[0], 0))
    flops = 2 * 2 * 1024 * 1152 * 128
    return pl.pallas_call(
        body,
        out_shape=shape,
        grid_spec=pltpu.PrefetchScalarGridSpec(
            num_scalar_prefetch=1, grid=(1,),
            in_specs=[
                heads,
                pl.BlockSpec((32, 1, TILE, BS), lambda i, m: (0, m[0], 0, 0)),
                part, part,
                pl.BlockSpec(memory_space=pl.ANY),
            ],
            out_specs=heads,
            scratch_shapes=[
                pltpu.VMEM((9 * BS, BS), jnp.bfloat16),
                pltpu.VMEM((9 * BS, 2 * BS), jnp.bfloat16),
                pltpu.VMEM((8, BS), jnp.float32),
            ],
        ),
        input_output_aliases={5: 0},
        cost_estimate=pl.CostEstimate(flops=flops, bytes_accessed=2 << 20, transcendentals=1024 * 1152),
        name="attend",
    )(meta, q, own, low, high, prev)


def blank_kernel(out):
    pass


def blank(like):
    return pl.pallas_call(
        blank_kernel,
        out_shape=jax.ShapeDtypeStruct(like.shape, like.dtype),
        out_specs=pl.BlockSpec(memory_space=pl.ANY),
        name="blank",
    )()


def local(n_head, queries, keys, values, ancestors, lengths):
    n_seq = 32
    place, level = lax.axis_index("seq"), lax.axis_index("head")
    pool, rank = pool_of(ancestors)
    pools = lax.all_to_all(jnp.broadcast_to(pool[None, None], (n_seq, 1, BS)), "seq", 0, 0, tiled=True)
    pools = pools.reshape(n_seq, BS)

    named = lax.dynamic_slice_in_dim(ancestors, level, 1)[0]
    ranks = lax.dynamic_slice_in_dim(rank, level, 1)[0]
    far_len = jnp.take(lengths, named)
    own_len = lax.dynamic_slice_in_dim(lengths, place * n_head + level, 1)

    def meta_of(g):
        return jnp.concatenate([g.astype(jnp.int32).reshape(1), ranks, far_len, own_len])

    own = jnp.concatenate([keys, values], axis=0).reshape(32, TILE, n_head, BS).transpose(0, 2, 1, 3)
    held = lax.all_to_all(own.reshape(n_seq * n_head, TILE, BS), ("seq", "head"), 0, 0, tiled=True)
    low, high = pick(pools, held)
    low = lax.all_to_all(low, "seq", 0, 0, tiled=True)
    high = lax.all_to_all(high, "seq", 0, 0, tiled=True)

    up = [(i, (i + 1) % n_head) for i in range(n_head)]
    down = [(i, (i - 1) % n_head) for i in range(n_head)]
    out = blank(queries)
    out = attend(meta_of(level), queries, own, low, high, out)
    low_up = low_down = low
    high_up = high_down = high
    for step in range(1, n_head // 2 + 1):
        last = step == n_head // 2
        low_up = lax.ppermute(low_up, "head", up)
        high_down = lax.ppermute(high_down, "head", down)
        if last:
            out = attend(meta_of(lax.rem(level + step, n_head)), queries, own, low_up, high_down, out)
            break
        high_up = lax.ppermute(high_up, "head", up)
        low_down = lax.ppermute(low_down, "head", down)
        out = attend(meta_of(lax.rem(level + n_head - step, n_head)), queries, own, low_up, high_up, out)
        out = attend(meta_of(lax.rem(level + step, n_head)), queries, own, low_down, high_down, out)
    return out


def solution(mesh):
    placed = (
        P(("seq", "head"), None, None),
        P(("seq", "head"), None, None),
        P(("seq", "head"), None, None),
        P("seq", None),
        P(),
    )
    body = functools.partial(local, mesh.shape["head"])
    return jax.shard_map(
        body, mesh=mesh, in_specs=placed, out_specs=P(("seq", "head"), None, None), check_vma=False
    )
```

```python
import functools
import math

import jax
import jax.numpy as jnp
from jax import lax
from jax.experimental import pallas as pl
from jax.experimental.pallas import tpu as pltpu
from jax.sharding import PartitionSpec as P


BS = 128
POOL = 12
HALF = POOL // 2
TILE = 8
NEG = -1e30


def pool_of(ancestors):
    flat = ancestors.reshape(-1)
    n = flat.shape[0]
    order = jnp.arange(n, dtype=jnp.int32)
    same = flat[:, None] == flat[None, :]
    repeat = jnp.any(same & (order[None, :] < order[:, None]), axis=1)
    first = ~repeat
    rank = jnp.sum((first[None, :] & (flat[None, :] < flat[:, None])).astype(jnp.int32), axis=1)
    slots = jnp.arange(BS, dtype=jnp.int32)
    hit = first[:, None] & (rank[:, None] == slots[None, :])
    pool = jnp.sum(jnp.where(hit, flat[:, None], 0), axis=0)
    return pool, rank.reshape(ancestors.shape)


def pick_kernel(pools, held, low, high):
    def one(s, carry):
        for i in range(HALF):
            low[s, i] = held[pools[s, i]]
            high[s, i] = held[pools[s, HALF + i]]
        return carry

    lax.fori_loop(0, pools.shape[0], one, 0, unroll=4)


def pick(pools, held):
    groups = pools.shape[0]
    part = jax.ShapeDtypeStruct((groups, HALF, TILE, BS), held.dtype)
    whole = pl.BlockSpec(memory_space=pltpu.VMEM)
    return pl.pallas_call(
        pick_kernel,
        out_shape=(part, part),
        grid_spec=pltpu.PrefetchScalarGridSpec(
            num_scalar_prefetch=1, grid=(1,),
            in_specs=[pl.BlockSpec(held.shape, lambda i, _: (0, 0, 0))],
            out_specs=[pl.BlockSpec(part.shape, lambda i, _: (0, 0, 0, 0))] * 2,
        ),
        name="pick",
    )(pools, held)


def attend_kernel(scale, meta, q, own, low, high, _, out, keys, vals, acc):
    far = 8
    row = lax.broadcasted_iota(jnp.int32, (BS, BS), 0)

    def put(j, k, v, length):
        k = k.astype(jnp.float32).reshape(BS, BS)
        v = v.astype(jnp.float32).reshape(BS, BS)
        valid = row < length
        at = slice(j * BS, (j + 1) * BS)
        keys[at, :] = jnp.where(valid, k, k[0:1, :]).astype(jnp.bfloat16)
        vals[at, 0:BS] = jnp.where(valid, v, 0.0).astype(jnp.bfloat16)
        vals[at, BS:] = jnp.where(valid, 1.0, 0.0).astype(jnp.bfloat16)

    put(0, own[0:16, 0], own[16:32, 0], meta[17])
    for j in range(far):
        place, length = meta[1 + j], meta[9 + j]

        @pl.when(place < HALF)
        def _():
            put(j + 1, low[0:16, place], low[16:32, place], length)

        @pl.when(place >= HALF)
        def _():
            put(j + 1, high[0:16, place - HALF], high[16:32, place - HALF], length)

    tokens = 32
    rows = tokens * 8
    token = lax.broadcasted_iota(jnp.int32, (rows, BS), 0) // 8
    offset = lax.broadcasted_iota(jnp.int32, (rows, BS), 1)
    for i in range(BS // tokens):
        at = slice(i * tokens, (i + 1) * tokens)
        qt = q[at].astype(jnp.float32).reshape(rows, BS).astype(jnp.bfloat16)
        s = lax.dot_general(qt, keys[...], (((1,), (1,)), ((), ())), preferred_element_type=jnp.float32)
        s_own = jnp.where(offset <= token + i * tokens, s[:, 0:BS], NEG)
        s_far = s[:, BS:]
        m = jnp.maximum(jnp.max(s_own, axis=1, keepdims=True), jnp.max(s_far, axis=1, keepdims=True))
        p_own = jnp.exp2((s_own - m) * scale).astype(jnp.bfloat16)
        p_far = jnp.exp2((s_far - m) * scale).astype(jnp.bfloat16)
        o = jnp.dot(p_own, vals[0:BS, :], preferred_element_type=jnp.float32)
        o = o + jnp.dot(p_far, vals[BS:, :], preferred_element_type=jnp.float32)
        r = o[:, 0:BS] / o[:, BS:]
        out[at] = r.reshape(tokens, 8, BS).astype(out.dtype)


def attend(meta, q, own, low, high, prev):
    scale = math.log2(math.e) / math.sqrt(BS)
    shape = jax.ShapeDtypeStruct(q.shape, q.dtype)
    body = functools.partial(attend_kernel, scale)
    part = pl.BlockSpec(low.shape, lambda i, m: (0, 0, 0, 0))
    heads = pl.BlockSpec((BS, 8, BS), lambda i, m: (0, m[0], 0))
    flops = 2 * 2 * 1024 * 1152 * 128
    return pl.pallas_call(
        body,
        out_shape=shape,
        grid_spec=pltpu.PrefetchScalarGridSpec(
            num_scalar_prefetch=1, grid=(1,),
            in_specs=[
                heads,
                pl.BlockSpec((32, 1, TILE, BS), lambda i, m: (0, m[0], 0, 0)),
                part, part,
                pl.BlockSpec(memory_space=pl.ANY),
            ],
            out_specs=heads,
            scratch_shapes=[
                pltpu.VMEM((9 * BS, BS), jnp.bfloat16),
                pltpu.VMEM((9 * BS, 2 * BS), jnp.bfloat16),
                pltpu.VMEM((8, BS), jnp.float32),
            ],
        ),
        input_output_aliases={5: 0},
        cost_estimate=pl.CostEstimate(flops=flops, bytes_accessed=2 << 20, transcendentals=1024 * 1152),
        name="attend",
    )(meta, q, own, low, high, prev)


def blank_kernel(out):
    pass


def blank(like):
    return pl.pallas_call(
        blank_kernel,
        out_shape=jax.ShapeDtypeStruct(like.shape, like.dtype),
        out_specs=pl.BlockSpec(memory_space=pl.ANY),
        name="blank",
    )()


def local(n_head, queries, keys, values, ancestors, lengths):
    return attention(n_head, queries, keys, values, ancestors, lengths)


def attention(n_head, queries, keys, values, ancestors, lengths):
    n_seq = 32
    place, level = lax.axis_index("seq"), lax.axis_index("head")
    pool, rank = pool_of(ancestors)
    pools = lax.all_to_all(jnp.broadcast_to(pool[None, None], (n_seq, 1, BS)), "seq", 0, 0, tiled=True)
    pools = jnp.minimum(pools.reshape(n_seq, BS), n_seq * n_head - 1)

    named = lax.dynamic_slice_in_dim(ancestors, level, 1)[0]
    ranks = lax.dynamic_slice_in_dim(rank, level, 1)[0]
    far_len = jnp.take(lengths, named)
    own_len = lax.dynamic_slice_in_dim(lengths, place * n_head + level, 1)

    def meta_of(g):
        return jnp.concatenate([g.astype(jnp.int32).reshape(1), ranks, far_len, own_len])

    own = jnp.concatenate([keys, values], axis=0).reshape(32, TILE, n_head, BS).transpose(0, 2, 1, 3)
    held = lax.all_to_all(own.reshape(n_seq * n_head, TILE, BS), ("seq", "head"), 0, 0, tiled=True)
    low, high = pick(pools, held)
    low = lax.all_to_all(low, "seq", 0, 0, tiled=True)
    high = lax.all_to_all(high, "seq", 0, 0, tiled=True)

    up = [(i, (i + 1) % n_head) for i in range(n_head)]
    down = [(i, (i - 1) % n_head) for i in range(n_head)]
    out = blank(queries)
    out = attend(meta_of(level), queries, own, low, high, out)
    low_up = low_down = low
    high_up = high_down = high
    for step in range(1, n_head // 2 + 1):
        last = step == n_head // 2
        low_up = lax.ppermute(low_up, "head", up)
        high_down = lax.ppermute(high_down, "head", down)
        if last:
            out = attend(meta_of(lax.rem(level + step, n_head)), queries, own, low_up, high_down, out)
            break
        high_up = lax.ppermute(high_up, "head", up)
        low_down = lax.ppermute(low_down, "head", down)
        out = attend(meta_of(lax.rem(level + n_head - step, n_head)), queries, own, low_up, high_up, out)
        out = attend(meta_of(lax.rem(level + step, n_head)), queries, own, low_down, high_down, out)
    return out


def solution(mesh):
    placed = (
        P(("seq", "head"), None, None),
        P(("seq", "head"), None, None),
        P(("seq", "head"), None, None),
        P("seq", None),
        P(),
    )
    body = functools.partial(local, mesh.shape["head"])
    return jax.shard_map(
        body, mesh=mesh, in_specs=placed, out_specs=P(("seq", "head"), None, None), check_vma=False
    )
```

```python
import functools
import math

import jax
import jax.numpy as jnp
from jax import lax
from jax.experimental import pallas as pl
from jax.experimental.pallas import tpu as pltpu
from jax.sharding import PartitionSpec as P


BS = 128
POOL = 12
HALF = POOL // 2
TILE = 8
NEG = -1e30
GRANT = 24 << 20


def pool_of(ancestors):
    flat = ancestors.reshape(-1)
    n = flat.shape[0]
    order = jnp.arange(n, dtype=jnp.int32)
    same = flat[:, None] == flat[None, :]
    repeat = jnp.any(same & (order[None, :] < order[:, None]), axis=1)
    first = ~repeat
    rank = jnp.sum((first[None, :] & (flat[None, :] < flat[:, None])).astype(jnp.int32), axis=1)
    slots = jnp.arange(BS, dtype=jnp.int32)
    hit = first[:, None] & (rank[:, None] == slots[None, :])
    pool = jnp.sum(jnp.where(hit, flat[:, None], 0), axis=0)
    return pool, rank.reshape(ancestors.shape)


def vmem():
    return pl.BlockSpec(memory_space=pltpu.VMEM)


def smem():
    return pl.BlockSpec(memory_space=pltpu.SMEM)


def pick_kernel(pools, me, held, low, high):
    mine = me[0]

    def one(s, carry):
        row = s ^ mine
        for i in range(HALF):
            low[s, i] = held[pools[row, i]]
            high[s, i] = held[pools[row, HALF + i]]
        return carry

    lax.fori_loop(0, pools.shape[0], one, 0, unroll=2)


def pick(pools, me, held):
    groups = pools.shape[0]
    part = jax.ShapeDtypeStruct((groups, HALF, TILE, BS), held.dtype)
    return pl.pallas_call(
        pick_kernel,
        out_shape=(part, part),
        in_specs=[smem(), smem(), vmem()],
        out_specs=(vmem(), vmem()),
        compiler_params=pltpu.CompilerParams(vmem_limit_bytes=GRANT),
        name="pick",
    )(pools, me, held)


def attend_kernel(scale, call, meta, q, own, low, high, _, out, keys, vals):
    far = 8
    row = lax.broadcasted_iota(jnp.int32, (BS, BS), 0)
    g = meta[call, 0]

    def put(j, k, v, length):
        k = k.astype(jnp.float32).reshape(BS, BS)
        v = v.astype(jnp.float32).reshape(BS, BS)
        valid = row < length
        at = slice(j * BS, (j + 1) * BS)
        keys[at, :] = jnp.where(valid, k, k[0:1, :]).astype(jnp.bfloat16)
        vals[at, 0:BS] = jnp.where(valid, v, 0.0).astype(jnp.bfloat16)
        vals[at, BS:] = jnp.where(valid, 1.0, 0.0).astype(jnp.bfloat16)

    put(0, own[0:16, g], own[16:32, g], meta[call, 17])
    for j in range(far):
        place, length = meta[call, 1 + j], meta[call, 9 + j]

        @pl.when(place < HALF)
        def _():
            put(j + 1, low[0:16, place], low[16:32, place], length)

        @pl.when(place >= HALF)
        def _():
            put(j + 1, high[0:16, place - HALF], high[16:32, place - HALF], length)

    tokens = 32
    rows = tokens * 8
    token = lax.broadcasted_iota(jnp.int32, (rows, BS), 0) // 8
    offset = lax.broadcasted_iota(jnp.int32, (rows, BS), 1)
    heads = pl.ds(pl.multiple_of(g * 8, 8), 8)
    for i in range(BS // tokens):
        at = slice(i * tokens, (i + 1) * tokens)
        qt = q[at, heads].astype(jnp.float32).reshape(rows, BS).astype(jnp.bfloat16)
        s = lax.dot_general(qt, keys[...], (((1,), (1,)), ((), ())), preferred_element_type=jnp.float32)
        s_own = jnp.where(offset <= token + i * tokens, s[:, 0:BS], NEG)
        s_far = s[:, BS:]
        m = jnp.maximum(jnp.max(s_own, axis=1, keepdims=True), jnp.max(s_far, axis=1, keepdims=True))
        p_own = jnp.exp2((s_own - m) * scale).astype(jnp.bfloat16)
        p_far = jnp.exp2((s_far - m) * scale).astype(jnp.bfloat16)
        o = jnp.dot(p_own, vals[0:BS, :], preferred_element_type=jnp.float32)
        o = o + jnp.dot(p_far, vals[BS:, :], preferred_element_type=jnp.float32)
        r = o[:, 0:BS] / o[:, BS:]
        out[at] = r.reshape(tokens, 8, BS).astype(out.dtype)


def attend(call, meta, q, own, low, high, prev):
    scale = math.log2(math.e) / math.sqrt(BS)
    shape = jax.ShapeDtypeStruct(prev.shape, q.dtype)
    heads = pl.BlockSpec((BS, 8, BS), lambda i, m: (0, m[call, 0], 0))
    flops = 2 * 2 * 1024 * 1152 * 128
    return pl.pallas_call(
        functools.partial(attend_kernel, scale, call),
        out_shape=shape,
        grid_spec=pltpu.PrefetchScalarGridSpec(
            num_scalar_prefetch=1, grid=(1,),
            in_specs=[vmem(), vmem(), vmem(), vmem(), pl.BlockSpec(memory_space=pl.ANY)],
            out_specs=heads,
            scratch_shapes=[
                pltpu.VMEM((9 * BS, BS), jnp.bfloat16),
                pltpu.VMEM((9 * BS, 2 * BS), jnp.bfloat16),
            ],
        ),
        input_output_aliases={5: 0},
        compiler_params=pltpu.CompilerParams(vmem_limit_bytes=GRANT),
        cost_estimate=pl.CostEstimate(flops=flops, bytes_accessed=2 << 20, transcendentals=1024 * 1152),
        name="attend",
    )(meta, q, own, low, high, prev)


def blank_kernel(out):
    pass


def blank(like):
    return pl.pallas_call(
        blank_kernel,
        out_shape=jax.ShapeDtypeStruct(like.shape, like.dtype),
        out_specs=pl.BlockSpec(memory_space=pl.ANY),
        name="blank",
    )()


def local(n_head, queries, keys, values, ancestors, lengths):
    return attention(n_head, queries, keys, values, ancestors, lengths)


def attention(n_head, queries, keys, values, ancestors, lengths):
    n_seq = 32
    place, level = lax.axis_index("seq"), lax.axis_index("head")
    pool, rank = pool_of(ancestors)
    pools = pool[None]
    bit = 1
    while bit < n_seq:
        other = lax.ppermute(pools, "seq", [(i, i ^ bit) for i in range(n_seq)])
        pools = jnp.concatenate([pools, other], axis=0)
        bit *= 2

    named = lax.dynamic_slice_in_dim(ancestors, level, 1)
    ranks = lax.dynamic_slice_in_dim(rank, level, 1)
    far_len = jnp.take(lengths, named)
    own_len = lax.dynamic_slice_in_dim(lengths, place * n_head + level, 1)[None]
    row = jnp.concatenate([ranks, far_len, own_len], axis=1)
    shifts = [0]
    for step in range(1, n_head // 2):
        shifts += [n_head - step, step]
    shifts.append(n_head // 2)
    heads = (level + jnp.array(shifts, jnp.int32)) % n_head
    meta = jnp.concatenate([heads[:, None], jnp.broadcast_to(row, (n_head, row.shape[1]))], axis=1)

    own = jnp.concatenate([keys, values], axis=0).reshape(32, TILE, n_head, BS).transpose(0, 2, 1, 3)
    held = lax.all_to_all(own.reshape(n_seq * n_head, TILE, BS), ("seq", "head"), 0, 0, tiled=True)
    low, high = pick(pools, place.astype(jnp.int32)[None], held)
    low = lax.all_to_all(low, "seq", 0, 0, tiled=True)
    high = lax.all_to_all(high, "seq", 0, 0, tiled=True)

    up = [(i, (i + 1) % n_head) for i in range(n_head)]
    down = [(i, (i - 1) % n_head) for i in range(n_head)]
    out = blank(queries)
    out = attend(0, meta, queries, own, low, high, out)
    low_up = low_down = low
    high_up = high_down = high
    for step in range(1, n_head // 2 + 1):
        last = step == n_head // 2
        low_up = lax.ppermute(low_up, "head", up)
        high_down = lax.ppermute(high_down, "head", down)
        if last:
            out = attend(n_head - 1, meta, queries, own, low_up, high_down, out)
            break
        high_up = lax.ppermute(high_up, "head", up)
        low_down = lax.ppermute(low_down, "head", down)
        out = attend(2 * step - 1, meta, queries, own, low_up, high_up, out)
        out = attend(2 * step, meta, queries, own, low_down, high_down, out)
    return out


def solution(mesh):
    placed = (
        P(("seq", "head"), None, None),
        P(("seq", "head"), None, None),
        P(("seq", "head"), None, None),
        P("seq", None),
        P(),
    )
    body = functools.partial(local, mesh.shape["head"])
    return jax.shard_map(
        body, mesh=mesh, in_specs=placed, out_specs=P(("seq", "head"), None, None), check_vma=False
    )
```

```python
import functools
import math

import jax
import jax.numpy as jnp
from jax import lax
from jax.experimental import pallas as pl
from jax.experimental.pallas import tpu as pltpu
from jax.sharding import PartitionSpec as P


BS = 128
POOL = 12
TILE = 8
NEG = -1e30
GRANT = 24 << 20


def pool_of(ancestors):
    flat = ancestors.reshape(-1)
    n = flat.shape[0]
    order = jnp.arange(n, dtype=jnp.int32)
    same = flat[:, None] == flat[None, :]
    repeat = jnp.any(same & (order[None, :] < order[:, None]), axis=1)
    first = ~repeat
    rank = jnp.sum((first[None, :] & (flat[None, :] < flat[:, None])).astype(jnp.int32), axis=1)
    slots = jnp.arange(BS, dtype=jnp.int32)
    hit = first[:, None] & (rank[:, None] == slots[None, :])
    pool = jnp.sum(jnp.where(hit, flat[:, None], 0), axis=0)
    return pool, rank.reshape(ancestors.shape)


def vmem():
    return pl.BlockSpec(memory_space=pltpu.VMEM)


def smem():
    return pl.BlockSpec(memory_space=pltpu.SMEM)


def pick_kernel(pools, me, held, out):
    mine = me[0]

    def one(s, carry):
        row = s ^ mine
        for i in range(POOL):
            out[s, i] = held[pools[row, i]]
        return carry

    lax.fori_loop(0, pools.shape[0], one, 0, unroll=2)


def pick(pools, me, held):
    return pl.pallas_call(
        pick_kernel,
        out_shape=jax.ShapeDtypeStruct((pools.shape[0], POOL, TILE, BS), held.dtype),
        in_specs=[smem(), smem(), vmem()],
        out_specs=vmem(),
        compiler_params=pltpu.CompilerParams(vmem_limit_bytes=GRANT),
        name="pick",
    )(pools, me, held)


def attend_kernel(scale, call, meta, q, own, far_k, far_v, _, out, keys, vals, held, sems):
    far = 8
    g = meta[call, 0]
    lane = lax.broadcasted_iota(jnp.int32, (1, BS), 1)
    keys[0:BS, :] = own[0:16, g].reshape(BS, BS)
    vals[0:BS, 0:BS] = own[16:32, g].reshape(BS, BS)
    bias = []
    for j in range(far):
        at = slice((j + 1) * BS, (j + 2) * BS)
        place = meta[call, 1 + j]
        keys[at, :] = far_k[0:16, place].reshape(BS, BS)
        vals[at, 0:BS] = far_v[0:16, place].reshape(BS, BS)
        bias.append(jnp.where(lane < meta[call, 9 + j], 0.0, NEG))
    vals[:, BS:] = jnp.ones((vals.shape[0], BS), jnp.bfloat16)

    tokens = 32
    rows = tokens * 8
    parts = BS // tokens
    token = lax.broadcasted_iota(jnp.int32, (rows, BS), 0) // 8
    offset = lax.broadcasted_iota(jnp.int32, (rows, BS), 1)
    inside = offset < meta[call, 17]
    heads = pl.ds(pl.multiple_of(g * 8, 8), 8)

    def leave(i):
        at = pl.ds(i * tokens, tokens)
        return pltpu.make_async_copy(held.at[at], out.at[at, heads], sems.at[i])

    for i in range(parts):
        at = slice(i * tokens, (i + 1) * tokens)
        qt = q[at, heads].astype(jnp.float32).reshape(rows, BS).astype(jnp.bfloat16)
        s = lax.dot_general(qt, keys[...], (((1,), (1,)), ((), ())), preferred_element_type=jnp.float32)
        s = [jnp.where((offset <= token + i * tokens) & inside, s[:, 0:BS], NEG)] + [
            s[:, (j + 1) * BS : (j + 2) * BS] + bias[j] for j in range(far)
        ]
        m = jnp.max(functools.reduce(jnp.maximum, s), axis=1, keepdims=True)
        p = jnp.concatenate([jnp.exp2((x - m) * scale).astype(jnp.bfloat16) for x in s], axis=1)
        o = jnp.dot(p, vals[...], preferred_element_type=jnp.float32)
        r = o[:, 0:BS] / o[:, BS:]
        held[at] = r.reshape(tokens, 8, BS).astype(out.dtype)
        leave(i).start()
    for i in range(parts):
        leave(i).wait()


def attend(call, meta, q, own, far_k, far_v, prev):
    scale = math.log2(math.e) / math.sqrt(BS)
    flops = 2 * 2 * 1024 * 1152 * 128
    hbm = pl.BlockSpec(memory_space=pl.ANY)
    return pl.pallas_call(
        functools.partial(attend_kernel, scale, call),
        out_shape=jax.ShapeDtypeStruct(prev.shape, q.dtype),
        in_specs=[smem(), vmem(), vmem(), vmem(), vmem(), hbm],
        out_specs=hbm,
        scratch_shapes=[
            pltpu.VMEM((9 * BS, BS), jnp.bfloat16),
            pltpu.VMEM((9 * BS, 2 * BS), jnp.bfloat16),
            pltpu.VMEM((BS, 8, BS), jnp.bfloat16),
            pltpu.SemaphoreType.DMA((4,)),
        ],
        input_output_aliases={5: 0},
        compiler_params=pltpu.CompilerParams(vmem_limit_bytes=GRANT),
        cost_estimate=pl.CostEstimate(flops=flops, bytes_accessed=2 << 20, transcendentals=1024 * 1152),
        name="attend",
    )(meta, q, own, far_k, far_v, prev)


def blank_kernel(out):
    pass


def blank(like):
    return pl.pallas_call(
        blank_kernel,
        out_shape=jax.ShapeDtypeStruct(like.shape, like.dtype),
        out_specs=pl.BlockSpec(memory_space=pl.ANY),
        name="blank",
    )()


def local(n_head, queries, keys, values, ancestors, lengths):
    return attention(n_head, queries, keys, values, ancestors, lengths)


def attention(n_head, queries, keys, values, ancestors, lengths):
    n_seq = 32
    place, level = lax.axis_index("seq"), lax.axis_index("head")
    pool, rank = pool_of(ancestors)
    pools = pool[None]
    bit = 1
    while bit < n_seq:
        other = lax.ppermute(pools, "seq", [(i, i ^ bit) for i in range(n_seq)])
        pools = jnp.concatenate([pools, other], axis=0)
        bit *= 2

    named = lax.dynamic_slice_in_dim(ancestors, level, 1)
    ranks = lax.dynamic_slice_in_dim(rank, level, 1)
    far_len = jnp.take(lengths, named)
    own_len = lax.dynamic_slice_in_dim(lengths, place * n_head + level, 1)[None]
    row = jnp.concatenate([ranks, far_len, own_len], axis=1)
    shifts = [0]
    for step in range(1, n_head // 2):
        shifts += [n_head - step, step]
    shifts.append(n_head // 2)
    heads = (level + jnp.array(shifts, jnp.int32)) % n_head
    meta = jnp.concatenate([heads[:, None], jnp.broadcast_to(row, (n_head, row.shape[1]))], axis=1)

    own = jnp.concatenate([keys, values], axis=0).reshape(32, TILE, n_head, BS).transpose(0, 2, 1, 3)
    held = lax.all_to_all(own.reshape(n_seq * n_head, TILE, BS), ("seq", "head"), 0, 0, tiled=True)
    picked = pick(pools, place.astype(jnp.int32)[None], held)
    far = lax.all_to_all(picked, "seq", 0, 0, tiled=True)
    far_k, far_v = far[:16], far[16:]

    up = [(i, (i + 1) % n_head) for i in range(n_head)]
    down = [(i, (i - 1) % n_head) for i in range(n_head)]
    out = blank(queries)
    out = attend(0, meta, queries, own, far_k, far_v, out)
    k_up = k_down = far_k
    v_up = v_down = far_v
    for step in range(1, n_head // 2 + 1):
        k_up = lax.ppermute(k_up, "head", up)
        v_down = lax.ppermute(v_down, "head", down)
        if step == n_head // 2:
            out = attend(n_head - 1, meta, queries, own, k_up, v_down, out)
            break
        v_up = lax.ppermute(v_up, "head", up)
        k_down = lax.ppermute(k_down, "head", down)
        out = attend(2 * step - 1, meta, queries, own, k_up, v_up, out)
        out = attend(2 * step, meta, queries, own, k_down, v_down, out)
    return out


def solution(mesh):
    placed = (
        P(("seq", "head"), None, None),
        P(("seq", "head"), None, None),
        P(("seq", "head"), None, None),
        P("seq", None),
        P(),
    )
    body = functools.partial(local, mesh.shape["head"])
    return jax.shard_map(
        body, mesh=mesh, in_specs=placed, out_specs=P(("seq", "head"), None, None), check_vma=False
    )
```

```python
import functools
import math

import jax
import jax.numpy as jnp
from jax import lax
from jax.experimental import pallas as pl
from jax.experimental.pallas import tpu as pltpu
from jax.sharding import PartitionSpec as P


BS = 128
POOL = 12
PIECES = BS // 8
ALL = POOL * PIECES
ROOM = 152
TILE = 8
NEG = -1e30
GRANT = 24 << 20


def pool_of(ancestors):
    flat = ancestors.reshape(-1)
    n = flat.shape[0]
    order = jnp.arange(n, dtype=jnp.int32)
    same = flat[:, None] == flat[None, :]
    repeat = jnp.any(same & (order[None, :] < order[:, None]), axis=1)
    first = ~repeat
    rank = jnp.sum((first[None, :] & (flat[None, :] < flat[:, None])).astype(jnp.int32), axis=1)
    slots = jnp.arange(BS, dtype=jnp.int32)
    hit = first[:, None] & (rank[:, None] == slots[None, :])
    pool = jnp.sum(jnp.where(hit, flat[:, None], 0), axis=0)
    return pool, rank.reshape(ancestors.shape)


def vmem():
    return pl.BlockSpec(memory_space=pltpu.VMEM)


def smem():
    return pl.BlockSpec(memory_space=pltpu.SMEM)


def pick_kernel(pools, me, held, out):
    mine = me[0]

    def one(s, carry):
        row = s ^ mine
        for i in range(POOL):
            out[s, i] = held[pools[row, i]]
        return carry

    lax.fori_loop(0, pools.shape[0], one, 0, unroll=2)


def pick(pools, me, held):
    return pl.pallas_call(
        pick_kernel,
        out_shape=jax.ShapeDtypeStruct((pools.shape[0], POOL, TILE, BS), held.dtype),
        in_specs=[smem(), smem(), vmem()],
        out_specs=vmem(),
        compiler_params=pltpu.CompilerParams(vmem_limit_bytes=GRANT),
        name="pick",
    )(pools, me, held)


def pack_kernel(offs, far, main_k, main_v, rest, all_k, all_v):
    zero = jnp.zeros(all_k.shape, all_k.dtype)
    all_k[...] = zero
    all_v[...] = zero
    for i in range(POOL):
        at = pl.ds(offs[i], PIECES)
        all_k[at] = far[0:PIECES, i]
        all_v[at] = far[PIECES : 2 * PIECES, i]
    all_k[pl.ds(offs[POOL], PIECES)] = zero[0:PIECES]
    all_v[pl.ds(offs[POOL], PIECES)] = zero[0:PIECES]
    main_k[...] = all_k[0:ROOM]
    main_v[...] = all_v[0:ROOM]
    rest[0] = all_k[ROOM:ALL]
    rest[1] = all_v[ROOM:ALL]


def pack(offs, far):
    part = jax.ShapeDtypeStruct((ROOM, TILE, BS), far.dtype)
    rest = jax.ShapeDtypeStruct((2, ALL - ROOM, TILE, BS), far.dtype)
    work = pltpu.VMEM((ALL + PIECES, TILE, BS), far.dtype)
    return pl.pallas_call(
        pack_kernel,
        out_shape=(part, part, rest),
        in_specs=[smem(), vmem()],
        out_specs=(vmem(), vmem(), vmem()),
        scratch_shapes=[work, work],
        compiler_params=pltpu.CompilerParams(vmem_limit_bytes=GRANT),
        name="pack",
    )(offs, far)


def attend_kernel(scale, call, meta, q, own, far_k, far_v, rest, _, out, keys, vals, held, all_k, all_v, sems):
    far = 8
    g = meta[call, 0]
    over = meta[call, 18]
    lane = lax.broadcasted_iota(jnp.int32, (1, BS), 1)
    keys[0:BS, :] = own[0:16, g].reshape(BS, BS)
    vals[0:BS, 0:BS] = own[16:32, g].reshape(BS, BS)

    def start(j, room):
        return jnp.minimum(meta[call, 1 + j], room - PIECES)

    def load(from_k, from_v, room):
        for j in range(far):
            at = slice((j + 1) * BS, (j + 2) * BS)
            pieces = pl.ds(start(j, room), PIECES)
            keys[at, :] = from_k[pieces].reshape(BS, BS)
            vals[at, 0:BS] = from_v[pieces].reshape(BS, BS)

    @pl.when(over == 0)
    def _():
        load(far_k, far_v, ROOM)

    @pl.when(over != 0)
    def _():
        more_k = pltpu.make_async_copy(rest.at[g, 0], all_k.at[ROOM:ALL], sems.at[4])
        more_v = pltpu.make_async_copy(rest.at[g, 1], all_v.at[ROOM:ALL], sems.at[5])
        more_k.start()
        more_v.start()
        all_k[0:ROOM] = far_k[...]
        all_v[0:ROOM] = far_v[...]
        more_k.wait()
        more_v.wait()
        load(all_k, all_v, ALL)

    room = jnp.where(over != 0, ALL, ROOM)
    bias = []
    for j in range(far):
        low = (meta[call, 1 + j] - start(j, room)) * TILE
        bias.append(jnp.where((lane >= low) & (lane < low + meta[call, 9 + j]), 0.0, NEG))
    vals[:, BS:] = jnp.ones((vals.shape[0], BS), jnp.bfloat16)

    tokens = 32
    rows = tokens * 8
    parts = BS // tokens
    token = lax.broadcasted_iota(jnp.int32, (rows, BS), 0) // 8
    offset = lax.broadcasted_iota(jnp.int32, (rows, BS), 1)
    inside = offset < meta[call, 17]
    heads = pl.ds(pl.multiple_of(g * 8, 8), 8)

    def leave(i):
        at = pl.ds(i * tokens, tokens)
        return pltpu.make_async_copy(held.at[at], out.at[at, heads], sems.at[i])

    for i in range(parts):
        at = slice(i * tokens, (i + 1) * tokens)
        qt = q[at, heads].astype(jnp.float32).reshape(rows, BS).astype(jnp.bfloat16)
        s = lax.dot_general(qt, keys[...], (((1,), (1,)), ((), ())), preferred_element_type=jnp.float32)
        s = [jnp.where((offset <= token + i * tokens) & inside, s[:, 0:BS], NEG)] + [
            s[:, (j + 1) * BS : (j + 2) * BS] + bias[j] for j in range(far)
        ]
        m = jnp.max(functools.reduce(jnp.maximum, s), axis=1, keepdims=True)
        p = jnp.concatenate([jnp.exp2((x - m) * scale).astype(jnp.bfloat16) for x in s], axis=1)
        o = jnp.dot(p, vals[...], preferred_element_type=jnp.float32)
        r = o[:, 0:BS] / o[:, BS:]
        held[at] = r.reshape(tokens, 8, BS).astype(out.dtype)
        leave(i).start()
    for i in range(parts):
        leave(i).wait()


def attend(call, meta, q, own, far_k, far_v, rest, prev):
    scale = math.log2(math.e) / math.sqrt(BS)
    flops = 2 * 2 * 1024 * 1152 * 128
    hbm = pl.BlockSpec(memory_space=pl.ANY)
    return pl.pallas_call(
        functools.partial(attend_kernel, scale, call),
        out_shape=jax.ShapeDtypeStruct(prev.shape, q.dtype),
        in_specs=[smem(), vmem(), vmem(), vmem(), vmem(), hbm, hbm],
        out_specs=hbm,
        scratch_shapes=[
            pltpu.VMEM((9 * BS, BS), jnp.bfloat16),
            pltpu.VMEM((9 * BS, 2 * BS), jnp.bfloat16),
            pltpu.VMEM((BS, 8, BS), jnp.bfloat16),
            pltpu.VMEM((ALL, TILE, BS), jnp.bfloat16),
            pltpu.VMEM((ALL, TILE, BS), jnp.bfloat16),
            pltpu.SemaphoreType.DMA((6,)),
        ],
        input_output_aliases={6: 0},
        compiler_params=pltpu.CompilerParams(vmem_limit_bytes=GRANT),
        cost_estimate=pl.CostEstimate(flops=flops, bytes_accessed=2 << 20, transcendentals=1024 * 1152),
        name="attend",
    )(meta, q, own, far_k, far_v, rest, prev)


def blank_kernel(out):
    pass


def blank(shape, dtype):
    return pl.pallas_call(
        blank_kernel,
        out_shape=jax.ShapeDtypeStruct(shape, dtype),
        out_specs=pl.BlockSpec(memory_space=pl.ANY),
        name="blank",
    )()


def local(n_head, queries, keys, values, ancestors, lengths):
    return attention(n_head, queries, keys, values, ancestors, lengths)


def attention(n_head, queries, keys, values, ancestors, lengths):
    n_seq = 32
    place, level = lax.axis_index("seq"), lax.axis_index("head")
    pool, rank = pool_of(ancestors)
    pools = pool[None]
    bit = 1
    while bit < n_seq:
        other = lax.ppermute(pools, "seq", [(i, i ^ bit) for i in range(n_seq)])
        pools = jnp.concatenate([pools, other], axis=0)
        bit *= 2

    named = lax.dynamic_slice_in_dim(ancestors, level, 1)
    ranks = lax.dynamic_slice_in_dim(rank, level, 1)
    far_len = jnp.take(lengths, named)
    own_len = lax.dynamic_slice_in_dim(lengths, place * n_head + level, 1)[None]
    count = (jnp.take(lengths, pool[:POOL]) + TILE - 1) // TILE
    slot = jnp.arange(POOL + 1, dtype=jnp.int32)
    offs = jnp.sum(jnp.where(slot[None, :POOL] < slot[:, None], count[None, :], 0), axis=1)
    over = offs[POOL] > ROOM
    far_off = jnp.sum(jnp.where(ranks.reshape(-1, 1) == slot[None, :POOL], offs[None, :POOL], 0), axis=1)[None]
    row = jnp.concatenate([far_off, far_len, own_len, over.astype(jnp.int32).reshape(1, 1)], axis=1)
    shifts = [0]
    for step in range(1, n_head // 2):
        shifts += [n_head - step, step]
    shifts.append(n_head // 2)
    heads = (level + jnp.array(shifts, jnp.int32)) % n_head
    meta = jnp.concatenate([heads[:, None], jnp.broadcast_to(row, (n_head, row.shape[1]))], axis=1)

    own = jnp.concatenate([keys, values], axis=0).reshape(32, TILE, n_head, BS).transpose(0, 2, 1, 3)
    held = lax.all_to_all(own.reshape(n_seq * n_head, TILE, BS), ("seq", "head"), 0, 0, tiled=True)
    picked = pick(pools, place.astype(jnp.int32)[None], held)
    far = lax.all_to_all(picked, "seq", 0, 0, tiled=True)
    far_k, far_v, rest = pack(offs, far)
    shape = (n_head,) + rest.shape
    rest = lax.cond(
        over,
        lambda r: lax.all_to_all(jnp.broadcast_to(r[None], shape), "head", 0, 0, tiled=True),
        lambda r: blank(shape, r.dtype),
        rest,
    )

    up = [(i, (i + 1) % n_head) for i in range(n_head)]
    down = [(i, (i - 1) % n_head) for i in range(n_head)]
    out = blank(queries.shape, queries.dtype)
    out = attend(0, meta, queries, own, far_k, far_v, rest, out)
    k_up = k_down = far_k
    v_up = v_down = far_v
    for step in range(1, n_head // 2 + 1):
        k_up = lax.ppermute(k_up, "head", up)
        v_down = lax.ppermute(v_down, "head", down)
        if step == n_head // 2:
            out = attend(n_head - 1, meta, queries, own, k_up, v_down, rest, out)
            break
        v_up = lax.ppermute(v_up, "head", up)
        k_down = lax.ppermute(k_down, "head", down)
        out = attend(2 * step - 1, meta, queries, own, k_up, v_up, rest, out)
        out = attend(2 * step, meta, queries, own, k_down, v_down, rest, out)
    return out


def solution(mesh):
    placed = (
        P(("seq", "head"), None, None),
        P(("seq", "head"), None, None),
        P(("seq", "head"), None, None),
        P("seq", None),
        P(),
    )
    body = functools.partial(local, mesh.shape["head"])
    return jax.shard_map(
        body, mesh=mesh, in_specs=placed, out_specs=P(("seq", "head"), None, None), check_vma=False
    )
```

```python
import functools
import math

import jax
import jax.numpy as jnp
from jax import lax
from jax.experimental import pallas as pl
from jax.experimental.pallas import tpu as pltpu
from jax.sharding import PartitionSpec as P


BS = 128
POOL = 12
PIECES = BS // 8
ALL = POOL * PIECES
ROOM = 152
TILE = 8
NEG = -1e30
GRANT = 24 << 20


def pool_of(ancestors):
    flat = ancestors.reshape(-1)
    n = flat.shape[0]
    order = jnp.arange(n, dtype=jnp.int32)
    same = flat[:, None] == flat[None, :]
    repeat = jnp.any(same & (order[None, :] < order[:, None]), axis=1)
    first = ~repeat
    rank = jnp.sum((first[None, :] & (flat[None, :] < flat[:, None])).astype(jnp.int32), axis=1)
    slots = jnp.arange(BS, dtype=jnp.int32)
    hit = first[:, None] & (rank[:, None] == slots[None, :])
    pool = jnp.sum(jnp.where(hit, flat[:, None], 0), axis=0)
    return pool, rank.reshape(ancestors.shape)


def vmem():
    return pl.BlockSpec(memory_space=pltpu.VMEM)


def smem():
    return pl.BlockSpec(memory_space=pltpu.SMEM)


def pick_kernel(pools, me, held, out):
    mine = me[0]

    def one(s, carry):
        row = s ^ mine
        for i in range(POOL):
            out[s, i] = held[pools[row, i]]
        return carry

    lax.fori_loop(0, pools.shape[0], one, 0, unroll=2)


def pick(pools, me, held):
    return pl.pallas_call(
        pick_kernel,
        out_shape=jax.ShapeDtypeStruct((pools.shape[0], POOL, TILE, BS), held.dtype),
        in_specs=[smem(), smem(), vmem()],
        out_specs=vmem(),
        compiler_params=pltpu.CompilerParams(vmem_limit_bytes=GRANT),
        name="pick",
    )(pools, me, held)


def pack_kernel(offs, far, main_k, main_v, rest, all_k, all_v):
    zero = jnp.zeros(all_k.shape, all_k.dtype)
    all_k[...] = zero
    all_v[...] = zero
    for i in range(POOL):
        at = pl.ds(offs[i], PIECES)
        all_k[at] = far[0:PIECES, i]
        all_v[at] = far[PIECES : 2 * PIECES, i]
    all_k[pl.ds(offs[POOL], PIECES)] = zero[0:PIECES]
    all_v[pl.ds(offs[POOL], PIECES)] = zero[0:PIECES]
    main_k[...] = all_k[0:ROOM]
    main_v[...] = all_v[0:ROOM]
    rest[0] = all_k[ROOM:ALL]
    rest[1] = all_v[ROOM:ALL]


def pack(offs, far):
    part = jax.ShapeDtypeStruct((ROOM, TILE, BS), far.dtype)
    rest = jax.ShapeDtypeStruct((2, ALL - ROOM, TILE, BS), far.dtype)
    work = pltpu.VMEM((ALL + PIECES, TILE, BS), far.dtype)
    return pl.pallas_call(
        pack_kernel,
        out_shape=(part, part, rest),
        in_specs=[smem(), vmem()],
        out_specs=(vmem(), vmem(), vmem()),
        scratch_shapes=[work, work],
        compiler_params=pltpu.CompilerParams(vmem_limit_bytes=GRANT),
        name="pack",
    )(offs, far)


def attend_kernel(scale, call, meta, q, own, far_k, far_v, rest, _, out, keys, vals, held, all_k, all_v, sems):
    far = 8
    g = meta[call, 0]
    over = meta[call, 18]
    lane = lax.broadcasted_iota(jnp.int32, (1, BS), 1)
    keys[0:BS, :] = own[0:16, g].reshape(BS, BS)
    vals[0:BS, 0:BS] = own[16:32, g].reshape(BS, BS)

    def start(j, room):
        return jnp.minimum(meta[call, 1 + j], room - PIECES)

    def load(from_k, from_v, room):
        for j in range(far):
            at = slice((j + 1) * BS, (j + 2) * BS)
            pieces = pl.ds(start(j, room), PIECES)
            keys[at, :] = from_k[pieces].reshape(BS, BS)
            vals[at, 0:BS] = from_v[pieces].reshape(BS, BS)

    @pl.when(over == 0)
    def _():
        load(far_k, far_v, ROOM)

    @pl.when(over != 0)
    def _():
        more_k = pltpu.make_async_copy(rest.at[g, 0], all_k.at[ROOM:ALL], sems.at[4])
        more_v = pltpu.make_async_copy(rest.at[g, 1], all_v.at[ROOM:ALL], sems.at[5])
        more_k.start()
        more_v.start()
        all_k[0:ROOM] = far_k[...]
        all_v[0:ROOM] = far_v[...]
        more_k.wait()
        more_v.wait()
        load(all_k, all_v, ALL)

    room = jnp.where(over != 0, ALL, ROOM)
    bias = []
    for j in range(far):
        low = (meta[call, 1 + j] - start(j, room)) * TILE
        bias.append(jnp.where((lane >= low) & (lane < low + meta[call, 9 + j]), 0.0, NEG))
    vals[:, BS:] = jnp.ones((vals.shape[0], BS), jnp.bfloat16)

    tokens = 32
    rows = tokens * 8
    parts = BS // tokens
    token = lax.broadcasted_iota(jnp.int32, (rows, BS), 0) // 8
    offset = lax.broadcasted_iota(jnp.int32, (rows, BS), 1)
    inside = offset < meta[call, 17]
    heads = pl.ds(pl.multiple_of(g * 8, 8), 8)

    def leave(i):
        at = pl.ds(i * tokens, tokens)
        return pltpu.make_async_copy(held.at[at], out.at[at, heads], sems.at[i])

    def scores(i):
        qt = q[g, i * tokens : (i + 1) * tokens].reshape(rows, BS)
        s = lax.dot_general(qt, keys[...], (((1,), (1,)), ((), ())), preferred_element_type=jnp.float32)
        return [jnp.where((offset <= token + i * tokens) & inside, s[:, 0:BS], NEG)] + [
            s[:, (j + 1) * BS : (j + 2) * BS] + bias[j] for j in range(far)
        ]

    def weights(s):
        m = jnp.max(functools.reduce(jnp.maximum, s), axis=1, keepdims=True) * scale
        return jnp.concatenate([jnp.exp2(x * scale - m).astype(jnp.bfloat16) for x in s], axis=1)

    every = [scores(i) for i in range(parts)]
    every = [weights(s) for s in every]
    for i in range(parts):
        o = jnp.dot(every[i], vals[...], preferred_element_type=jnp.float32)
        r = o[:, 0:BS] / o[:, BS:]
        held[i * tokens : (i + 1) * tokens] = r.reshape(tokens, 8, BS).astype(out.dtype)
        leave(i).start()
    for i in range(parts):
        leave(i).wait()


def attend(call, meta, q, own, far_k, far_v, rest, prev):
    scale = math.log2(math.e) / math.sqrt(BS)
    flops = 2 * 2 * 1024 * 1152 * 128
    hbm = pl.BlockSpec(memory_space=pl.ANY)
    return pl.pallas_call(
        functools.partial(attend_kernel, scale, call),
        out_shape=jax.ShapeDtypeStruct(prev.shape, prev.dtype),
        in_specs=[smem(), vmem(), vmem(), vmem(), vmem(), hbm, hbm],
        out_specs=hbm,
        scratch_shapes=[
            pltpu.VMEM((9 * BS, BS), jnp.bfloat16),
            pltpu.VMEM((9 * BS, 2 * BS), jnp.bfloat16),
            pltpu.VMEM((BS, 8, BS), jnp.bfloat16),
            pltpu.VMEM((ALL, TILE, BS), jnp.bfloat16),
            pltpu.VMEM((ALL, TILE, BS), jnp.bfloat16),
            pltpu.SemaphoreType.DMA((6,)),
        ],
        input_output_aliases={6: 0},
        compiler_params=pltpu.CompilerParams(vmem_limit_bytes=GRANT),
        cost_estimate=pl.CostEstimate(flops=flops, bytes_accessed=2 << 20, transcendentals=1024 * 1152),
        name="attend",
    )(meta, q, own, far_k, far_v, rest, prev)


def stage_kernel(q, out, sems):
    copies = [pltpu.make_async_copy(q.at[:, h * 8 : (h + 1) * 8], out.at[h], sems.at[h]) for h in range(8)]
    for copy in copies:
        copy.start()
    for copy in copies:
        copy.wait()


def stage(q):
    return pl.pallas_call(
        stage_kernel,
        out_shape=jax.ShapeDtypeStruct((8, BS, 8, BS), q.dtype),
        in_specs=[pl.BlockSpec(memory_space=pl.ANY)],
        out_specs=vmem(),
        scratch_shapes=[pltpu.SemaphoreType.DMA((8,))],
        compiler_params=pltpu.CompilerParams(vmem_limit_bytes=GRANT),
        name="stage",
    )(q)


def blank_kernel(out):
    pass


def blank(shape, dtype):
    return pl.pallas_call(
        blank_kernel,
        out_shape=jax.ShapeDtypeStruct(shape, dtype),
        out_specs=pl.BlockSpec(memory_space=pl.ANY),
        name="blank",
    )()


def local(n_head, queries, keys, values, ancestors, lengths):
    return attention(n_head, queries, keys, values, ancestors, lengths)


def attention(n_head, queries, keys, values, ancestors, lengths):
    n_seq = 32
    place, level = lax.axis_index("seq"), lax.axis_index("head")
    pool, rank = pool_of(ancestors)
    pools = pool[None]
    bit = 1
    while bit < n_seq:
        other = lax.ppermute(pools, "seq", [(i, i ^ bit) for i in range(n_seq)])
        pools = jnp.concatenate([pools, other], axis=0)
        bit *= 2

    named = lax.dynamic_slice_in_dim(ancestors, level, 1)
    ranks = lax.dynamic_slice_in_dim(rank, level, 1)
    far_len = jnp.take(lengths, named)
    own_len = lax.dynamic_slice_in_dim(lengths, place * n_head + level, 1)[None]
    count = (jnp.take(lengths, pool[:POOL]) + TILE - 1) // TILE
    slot = jnp.arange(POOL + 1, dtype=jnp.int32)
    offs = jnp.sum(jnp.where(slot[None, :POOL] < slot[:, None], count[None, :], 0), axis=1)
    over = offs[POOL] > ROOM
    far_off = jnp.sum(jnp.where(ranks.reshape(-1, 1) == slot[None, :POOL], offs[None, :POOL], 0), axis=1)[None]
    row = jnp.concatenate([far_off, far_len, own_len, over.astype(jnp.int32).reshape(1, 1)], axis=1)
    shifts = [0]
    for step in range(1, n_head // 2):
        shifts += [n_head - step, step]
    shifts.append(n_head // 2)
    heads = (level + jnp.array(shifts, jnp.int32)) % n_head
    meta = jnp.concatenate([heads[:, None], jnp.broadcast_to(row, (n_head, row.shape[1]))], axis=1)

    own = jnp.concatenate([keys, values], axis=0).reshape(32, TILE, n_head, BS).transpose(0, 2, 1, 3)
    held = lax.all_to_all(own.reshape(n_seq * n_head, TILE, BS), ("seq", "head"), 0, 0, tiled=True)
    picked = pick(pools, place.astype(jnp.int32)[None], held)
    far = lax.all_to_all(picked, "seq", 0, 0, tiled=True)
    far_k, far_v, rest = pack(offs, far)
    shape = (n_head,) + rest.shape
    rest = lax.cond(
        over,
        lambda r: lax.all_to_all(jnp.broadcast_to(r[None], shape), "head", 0, 0, tiled=True),
        lambda r: blank(shape, r.dtype),
        rest,
    )

    up = [(i, (i + 1) % n_head) for i in range(n_head)]
    down = [(i, (i - 1) % n_head) for i in range(n_head)]
    out = blank(queries.shape, queries.dtype)
    queries = stage(queries)
    out = attend(0, meta, queries, own, far_k, far_v, rest, out)
    k_up = k_down = far_k
    v_up = v_down = far_v
    for step in range(1, n_head // 2 + 1):
        k_up = lax.ppermute(k_up, "head", up)
        v_down = lax.ppermute(v_down, "head", down)
        if step == n_head // 2:
            out = attend(n_head - 1, meta, queries, own, k_up, v_down, rest, out)
            break
        v_up = lax.ppermute(v_up, "head", up)
        k_down = lax.ppermute(k_down, "head", down)
        out = attend(2 * step - 1, meta, queries, own, k_up, v_up, rest, out)
        out = attend(2 * step, meta, queries, own, k_down, v_down, rest, out)
    return out


def solution(mesh):
    placed = (
        P(("seq", "head"), None, None),
        P(("seq", "head"), None, None),
        P(("seq", "head"), None, None),
        P("seq", None),
        P(),
    )
    body = functools.partial(local, mesh.shape["head"])
    return jax.shard_map(
        body, mesh=mesh, in_specs=placed, out_specs=P(("seq", "head"), None, None), check_vma=False
    )
```

```python
import functools
import math

import jax
import jax.numpy as jnp
from jax import lax
from jax.experimental import pallas as pl
from jax.experimental.pallas import tpu as pltpu
from jax.sharding import PartitionSpec as P


BS = 128
POOL = 12
PIECES = BS // 8
ALL = POOL * PIECES
ROOM = 152
TILE = 8
NEG = -1e30
GRANT = 24 << 20


def pool_of(ancestors):
    flat = ancestors.reshape(-1)
    n = flat.shape[0]
    order = jnp.arange(n, dtype=jnp.int32)
    same = flat[:, None] == flat[None, :]
    repeat = jnp.any(same & (order[None, :] < order[:, None]), axis=1)
    first = ~repeat
    rank = jnp.sum((first[None, :] & (flat[None, :] < flat[:, None])).astype(jnp.int32), axis=1)
    slots = jnp.arange(BS, dtype=jnp.int32)
    hit = first[:, None] & (rank[:, None] == slots[None, :])
    pool = jnp.sum(jnp.where(hit, flat[:, None], 0), axis=0)
    return pool, rank.reshape(ancestors.shape)


def vmem():
    return pl.BlockSpec(memory_space=pltpu.VMEM)


def smem():
    return pl.BlockSpec(memory_space=pltpu.SMEM)


def pick_kernel(pools, me, held, out):
    mine = me[0]

    def one(s, carry):
        row = s ^ mine
        for i in range(POOL):
            out[s, i] = held[pools[row, i]]
        return carry

    lax.fori_loop(0, pools.shape[0], one, 0, unroll=2)


def pick(pools, me, held):
    return pl.pallas_call(
        pick_kernel,
        out_shape=jax.ShapeDtypeStruct((pools.shape[0], POOL, TILE, BS), held.dtype),
        in_specs=[smem(), smem(), vmem()],
        out_specs=vmem(),
        compiler_params=pltpu.CompilerParams(vmem_limit_bytes=GRANT),
        name="pick",
    )(pools, me, held)


def pack_kernel(offs, far, main_k, main_v, rest, all_k, all_v):
    zero = jnp.zeros(all_k.shape, all_k.dtype)
    all_k[...] = zero
    all_v[...] = zero
    for i in range(POOL):
        at = pl.ds(offs[i], PIECES)
        all_k[at] = far[0:PIECES, i]
        all_v[at] = far[PIECES : 2 * PIECES, i]
    all_k[pl.ds(offs[POOL], PIECES)] = zero[0:PIECES]
    all_v[pl.ds(offs[POOL], PIECES)] = zero[0:PIECES]
    main_k[...] = all_k[0:ROOM]
    main_v[...] = all_v[0:ROOM]
    rest[0] = all_k[ROOM:ALL]
    rest[1] = all_v[ROOM:ALL]


def pack(offs, far):
    part = jax.ShapeDtypeStruct((ROOM, TILE, BS), far.dtype)
    rest = jax.ShapeDtypeStruct((2, ALL - ROOM, TILE, BS), far.dtype)
    work = pltpu.VMEM((ALL + PIECES, TILE, BS), far.dtype)
    return pl.pallas_call(
        pack_kernel,
        out_shape=(part, part, rest),
        in_specs=[smem(), vmem()],
        out_specs=(vmem(), vmem(), vmem()),
        scratch_shapes=[work, work],
        compiler_params=pltpu.CompilerParams(vmem_limit_bytes=GRANT),
        name="pack",
    )(offs, far)


def attend_kernel(scale, call, meta, q, own, far_k, far_v, rest, _, out, keys, vals, held, all_k, all_v, sems):
    far = 8
    g = meta[call, 0]
    over = meta[call, 18]
    lane = lax.broadcasted_iota(jnp.int32, (1, BS), 1)
    keys[0:BS, :] = own[0:16, g].reshape(BS, BS)
    vals[0:BS, :] = own[16:32, g].reshape(BS, BS)

    def start(j, room):
        return jnp.minimum(meta[call, 1 + j], room - PIECES)

    def load(from_k, from_v, room):
        for j in range(far):
            at = slice((j + 1) * BS, (j + 2) * BS)
            pieces = pl.ds(start(j, room), PIECES)
            keys[at, :] = from_k[pieces].reshape(BS, BS)
            vals[at, :] = from_v[pieces].reshape(BS, BS)

    @pl.when(over == 0)
    def _():
        load(far_k, far_v, ROOM)

    @pl.when(over != 0)
    def _():
        more_k = pltpu.make_async_copy(rest.at[g, 0], all_k.at[ROOM:ALL], sems.at[4])
        more_v = pltpu.make_async_copy(rest.at[g, 1], all_v.at[ROOM:ALL], sems.at[5])
        more_k.start()
        more_v.start()
        all_k[0:ROOM] = far_k[...]
        all_v[0:ROOM] = far_v[...]
        more_k.wait()
        more_v.wait()
        load(all_k, all_v, ALL)

    room = jnp.where(over != 0, ALL, ROOM)
    bias = []
    for j in range(far):
        low = (meta[call, 1 + j] - start(j, room)) * TILE
        bias.append(jnp.where((lane >= low) & (lane < low + meta[call, 9 + j]), 0.0, NEG))

    tokens = 32
    rows = tokens * 8
    parts = BS // tokens
    token = lax.broadcasted_iota(jnp.int32, (rows, BS), 0) // 8
    offset = lax.broadcasted_iota(jnp.int32, (rows, BS), 1)
    inside = offset < meta[call, 17]
    heads = pl.ds(pl.multiple_of(g * 8, 8), 8)

    def leave(i):
        at = pl.ds(i * tokens, tokens)
        return pltpu.make_async_copy(held.at[at], out.at[at, heads], sems.at[i])

    def scores(i):
        qt = q[g, i * tokens : (i + 1) * tokens].reshape(rows, BS)
        s = lax.dot_general(qt, keys[...], (((1,), (1,)), ((), ())), preferred_element_type=jnp.float32)
        return [jnp.where((offset <= token + i * tokens) & inside, s[:, 0:BS], NEG)] + [
            s[:, (j + 1) * BS : (j + 2) * BS] + bias[j] for j in range(far)
        ]

    def weights(s):
        m = jnp.max(functools.reduce(jnp.maximum, s), axis=1, keepdims=True) * scale
        return jnp.concatenate([jnp.exp2(x * scale - m).astype(jnp.bfloat16) for x in s], axis=1)

    every = [scores(i) for i in range(parts)]
    every = [weights(s) for s in every]
    wide = jnp.concatenate([vals[...], jnp.ones((9 * BS, BS), jnp.bfloat16)], axis=1)
    for i in range(parts):
        o = jnp.dot(every[i], wide, preferred_element_type=jnp.float32)
        r = o[:, 0:BS] / o[:, BS:]
        held[i * tokens : (i + 1) * tokens] = r.reshape(tokens, 8, BS).astype(out.dtype)
        leave(i).start()
    for i in range(parts):
        leave(i).wait()


def attend(call, meta, q, own, far_k, far_v, rest, prev):
    scale = math.log2(math.e) / math.sqrt(BS)
    flops = 2 * 2 * 1024 * 1152 * 128
    hbm = pl.BlockSpec(memory_space=pl.ANY)
    return pl.pallas_call(
        functools.partial(attend_kernel, scale, call),
        out_shape=jax.ShapeDtypeStruct(prev.shape, prev.dtype),
        in_specs=[smem(), vmem(), vmem(), vmem(), vmem(), hbm, hbm],
        out_specs=hbm,
        scratch_shapes=[
            pltpu.VMEM((9 * BS, BS), jnp.bfloat16),
            pltpu.VMEM((9 * BS, BS), jnp.bfloat16),
            pltpu.VMEM((BS, 8, BS), jnp.bfloat16),
            pltpu.VMEM((ALL, TILE, BS), jnp.bfloat16),
            pltpu.VMEM((ALL, TILE, BS), jnp.bfloat16),
            pltpu.SemaphoreType.DMA((6,)),
        ],
        input_output_aliases={6: 0},
        compiler_params=pltpu.CompilerParams(vmem_limit_bytes=GRANT),
        cost_estimate=pl.CostEstimate(flops=flops, bytes_accessed=2 << 20, transcendentals=1024 * 1152),
        name="attend",
    )(meta, q, own, far_k, far_v, rest, prev)


def stage_kernel(q, out, sems):
    copies = [pltpu.make_async_copy(q.at[:, h * 8 : (h + 1) * 8], out.at[h], sems.at[h]) for h in range(8)]
    for copy in copies:
        copy.start()
    for copy in copies:
        copy.wait()


def stage(q):
    return pl.pallas_call(
        stage_kernel,
        out_shape=jax.ShapeDtypeStruct((8, BS, 8, BS), q.dtype),
        in_specs=[pl.BlockSpec(memory_space=pl.ANY)],
        out_specs=vmem(),
        scratch_shapes=[pltpu.SemaphoreType.DMA((8,))],
        compiler_params=pltpu.CompilerParams(vmem_limit_bytes=GRANT),
        name="stage",
    )(q)


def blank_kernel(out):
    pass


def blank(shape, dtype):
    return pl.pallas_call(
        blank_kernel,
        out_shape=jax.ShapeDtypeStruct(shape, dtype),
        out_specs=pl.BlockSpec(memory_space=pl.ANY),
        name="blank",
    )()


def local(n_head, queries, keys, values, ancestors, lengths):
    return attention(n_head, queries, keys, values, ancestors, lengths)


def attention(n_head, queries, keys, values, ancestors, lengths):
    n_seq = 32
    place, level = lax.axis_index("seq"), lax.axis_index("head")
    pool, rank = pool_of(ancestors)
    pools = pool[None]
    bit = 1
    while bit < n_seq:
        other = lax.ppermute(pools, "seq", [(i, i ^ bit) for i in range(n_seq)])
        pools = jnp.concatenate([pools, other], axis=0)
        bit *= 2

    named = lax.dynamic_slice_in_dim(ancestors, level, 1)
    ranks = lax.dynamic_slice_in_dim(rank, level, 1)
    far_len = jnp.take(lengths, named)
    own_len = lax.dynamic_slice_in_dim(lengths, place * n_head + level, 1)[None]
    count = (jnp.take(lengths, pool[:POOL]) + TILE - 1) // TILE
    slot = jnp.arange(POOL + 1, dtype=jnp.int32)
    offs = jnp.sum(jnp.where(slot[None, :POOL] < slot[:, None], count[None, :], 0), axis=1)
    over = offs[POOL] > ROOM
    far_off = jnp.sum(jnp.where(ranks.reshape(-1, 1) == slot[None, :POOL], offs[None, :POOL], 0), axis=1)[None]
    row = jnp.concatenate([far_off, far_len, own_len, over.astype(jnp.int32).reshape(1, 1)], axis=1)
    shifts = [0]
    for step in range(1, n_head // 2):
        shifts += [n_head - step, step]
    shifts.append(n_head // 2)
    heads = (level + jnp.array(shifts, jnp.int32)) % n_head
    meta = jnp.concatenate([heads[:, None], jnp.broadcast_to(row, (n_head, row.shape[1]))], axis=1)

    own = jnp.concatenate([keys, values], axis=0).reshape(32, TILE, n_head, BS).transpose(0, 2, 1, 3)
    held = lax.all_to_all(own.reshape(n_seq * n_head, TILE, BS), ("seq", "head"), 0, 0, tiled=True)
    picked = pick(pools, place.astype(jnp.int32)[None], held)
    far = lax.all_to_all(picked, "seq", 0, 0, tiled=True)
    far_k, far_v, rest = pack(offs, far)
    shape = (n_head,) + rest.shape
    rest = lax.cond(
        over,
        lambda r: lax.all_to_all(jnp.broadcast_to(r[None], shape), "head", 0, 0, tiled=True),
        lambda r: blank(shape, r.dtype),
        rest,
    )

    up = [(i, (i + 1) % n_head) for i in range(n_head)]
    down = [(i, (i - 1) % n_head) for i in range(n_head)]
    out = blank(queries.shape, queries.dtype)
    queries = stage(queries)
    out = attend(0, meta, queries, own, far_k, far_v, rest, out)
    k_up = k_down = far_k
    v_up = v_down = far_v
    for step in range(1, n_head // 2 + 1):
        k_up = lax.ppermute(k_up, "head", up)
        v_down = lax.ppermute(v_down, "head", down)
        if step == n_head // 2:
            out = attend(n_head - 1, meta, queries, own, k_up, v_down, rest, out)
            break
        v_up = lax.ppermute(v_up, "head", up)
        k_down = lax.ppermute(k_down, "head", down)
        out = attend(2 * step - 1, meta, queries, own, k_up, v_up, rest, out)
        out = attend(2 * step, meta, queries, own, k_down, v_down, rest, out)
    return out


def solution(mesh):
    placed = (
        P(("seq", "head"), None, None),
        P(("seq", "head"), None, None),
        P(("seq", "head"), None, None),
        P("seq", None),
        P(),
    )
    body = functools.partial(local, mesh.shape["head"])
    return jax.shard_map(
        body, mesh=mesh, in_specs=placed, out_specs=P(("seq", "head"), None, None), check_vma=False
    )
```

```python
import functools
import math

import jax
import jax.numpy as jnp
from jax import lax
from jax.experimental import pallas as pl
from jax.experimental.pallas import tpu as pltpu
from jax.sharding import PartitionSpec as P


BS = 128
POOL = 12
PIECES = BS // 8
ALL = POOL * PIECES
ROOM = 152
TILE = 8
NEG = -1e30
GRANT = 24 << 20


def pool_of(ancestors):
    flat = ancestors.reshape(-1)
    n = flat.shape[0]
    order = jnp.arange(n, dtype=jnp.int32)
    same = flat[:, None] == flat[None, :]
    repeat = jnp.any(same & (order[None, :] < order[:, None]), axis=1)
    first = ~repeat
    rank = jnp.sum((first[None, :] & (flat[None, :] < flat[:, None])).astype(jnp.int32), axis=1)
    slots = jnp.arange(BS, dtype=jnp.int32)
    hit = first[:, None] & (rank[:, None] == slots[None, :])
    pool = jnp.sum(jnp.where(hit, flat[:, None], 0), axis=0)
    return pool, rank.reshape(ancestors.shape)


def vmem():
    return pl.BlockSpec(memory_space=pltpu.VMEM)


def smem():
    return pl.BlockSpec(memory_space=pltpu.SMEM)


def pick_kernel(pools, me, held, out):
    mine = me[0]

    def one(s, carry):
        row = s ^ mine
        for i in range(POOL):
            out[s, i] = held[pools[row, i]]
        return carry

    lax.fori_loop(0, pools.shape[0], one, 0, unroll=2)


def pick(pools, me, held):
    return pl.pallas_call(
        pick_kernel,
        out_shape=jax.ShapeDtypeStruct((pools.shape[0], POOL, TILE, BS), held.dtype),
        in_specs=[smem(), smem(), vmem()],
        out_specs=vmem(),
        compiler_params=pltpu.CompilerParams(vmem_limit_bytes=GRANT),
        name="pick",
    )(pools, me, held)


def pack_kernel(offs, far, main_k, main_v, rest, all_k, all_v):
    zero = jnp.zeros(all_k.shape, all_k.dtype)
    all_k[...] = zero
    all_v[...] = zero
    for i in range(POOL):
        at = pl.ds(offs[i], PIECES)
        all_k[at] = far[0:PIECES, i]
        all_v[at] = far[PIECES : 2 * PIECES, i]
    all_k[pl.ds(offs[POOL], PIECES)] = zero[0:PIECES]
    all_v[pl.ds(offs[POOL], PIECES)] = zero[0:PIECES]
    main_k[...] = all_k[0:ROOM]
    main_v[...] = all_v[0:ROOM]
    rest[0] = all_k[ROOM:ALL]
    rest[1] = all_v[ROOM:ALL]


def pack(offs, far):
    part = jax.ShapeDtypeStruct((ROOM, TILE, BS), far.dtype)
    rest = jax.ShapeDtypeStruct((2, ALL - ROOM, TILE, BS), far.dtype)
    work = pltpu.VMEM((ALL + PIECES, TILE, BS), far.dtype)
    return pl.pallas_call(
        pack_kernel,
        out_shape=(part, part, rest),
        in_specs=[smem(), vmem()],
        out_specs=(vmem(), vmem(), vmem()),
        scratch_shapes=[work, work],
        compiler_params=pltpu.CompilerParams(vmem_limit_bytes=GRANT),
        name="pack",
    )(offs, far)


def attend_kernel(scale, call, meta, q, own, far_k, far_v, rest, _, out, keys, vals, held, all_k, all_v, sems):
    far = 8
    g = meta[call, 0]
    over = meta[call, 18]
    lane = lax.broadcasted_iota(jnp.int32, (1, BS), 1)
    keys[0:BS, :] = own[0:16, g].reshape(BS, BS)
    vals[0:BS, :] = own[16:32, g].reshape(BS, BS)

    def start(j, room):
        return jnp.minimum(meta[call, 1 + j], room - PIECES)

    def load(from_k, from_v, room):
        for j in range(far):
            at = slice((j + 1) * BS, (j + 2) * BS)
            pieces = pl.ds(start(j, room), PIECES)
            keys[at, :] = from_k[pieces].reshape(BS, BS)
            vals[at, :] = from_v[pieces].reshape(BS, BS)

    @pl.when(over == 0)
    def _():
        load(far_k, far_v, ROOM)

    @pl.when(over != 0)
    def _():
        more_k = pltpu.make_async_copy(rest.at[g, 0], all_k.at[ROOM:ALL], sems.at[4])
        more_v = pltpu.make_async_copy(rest.at[g, 1], all_v.at[ROOM:ALL], sems.at[5])
        more_k.start()
        more_v.start()
        all_k[0:ROOM] = far_k[...]
        all_v[0:ROOM] = far_v[...]
        more_k.wait()
        more_v.wait()
        load(all_k, all_v, ALL)

    room = jnp.where(over != 0, ALL, ROOM)
    bias = []
    for j in range(far):
        low = (meta[call, 1 + j] - start(j, room)) * TILE
        bias.append(jnp.where((lane >= low) & (lane < low + meta[call, 9 + j]), 0.0, NEG))

    tokens = 32
    rows = tokens * 8
    parts = BS // tokens
    token = lax.broadcasted_iota(jnp.int32, (rows, BS), 0) // 8
    offset = lax.broadcasted_iota(jnp.int32, (rows, BS), 1)
    inside = offset < meta[call, 17]
    heads = pl.ds(pl.multiple_of(g * 8, 8), 8)

    def leave(i):
        at = pl.ds(i * tokens, tokens)
        return pltpu.make_async_copy(held.at[at], out.at[at, heads], sems.at[i])

    def scores(i):
        qt = q[g, i * tokens : (i + 1) * tokens].reshape(rows, BS)
        s = lax.dot_general(qt, keys[...], (((1,), (1,)), ((), ())), preferred_element_type=jnp.float32)
        return [jnp.where((offset <= token + i * tokens) & inside, s[:, 0:BS], NEG)] + [
            s[:, (j + 1) * BS : (j + 2) * BS] + bias[j] for j in range(far)
        ]

    def weights(s):
        m = jnp.max(functools.reduce(jnp.maximum, s), axis=1, keepdims=True) * scale
        return jnp.concatenate([jnp.exp2(x * scale - m).astype(jnp.bfloat16) for x in s], axis=1)

    every = [scores(i) for i in range(parts)]
    every = [weights(s) for s in every]
    wide = jnp.concatenate([vals[...], jnp.ones((9 * BS, BS), jnp.bfloat16)], axis=1)
    for i in range(parts):
        o = jnp.dot(every[i], wide, preferred_element_type=jnp.float32)
        r = o[:, 0:BS] / o[:, BS:]
        held[i * tokens : (i + 1) * tokens] = r.reshape(tokens, 8, BS).astype(out.dtype)
        leave(i).start()
    for i in range(parts):
        leave(i).wait()


def attend(call, meta, q, own, far_k, far_v, rest, prev):
    scale = math.log2(math.e) / math.sqrt(BS)
    flops = 2 * 2 * 1024 * 1152 * 128
    hbm = pl.BlockSpec(memory_space=pl.ANY)
    return pl.pallas_call(
        functools.partial(attend_kernel, scale, call),
        out_shape=jax.ShapeDtypeStruct(prev.shape, prev.dtype),
        in_specs=[smem(), vmem(), vmem(), vmem(), vmem(), hbm, hbm],
        out_specs=hbm,
        scratch_shapes=[
            pltpu.VMEM((9 * BS, BS), jnp.bfloat16),
            pltpu.VMEM((9 * BS, BS), jnp.bfloat16),
            pltpu.VMEM((BS, 8, BS), jnp.bfloat16),
            pltpu.VMEM((ALL, TILE, BS), jnp.bfloat16),
            pltpu.VMEM((ALL, TILE, BS), jnp.bfloat16),
            pltpu.SemaphoreType.DMA((6,)),
        ],
        input_output_aliases={6: 0},
        compiler_params=pltpu.CompilerParams(vmem_limit_bytes=GRANT),
        cost_estimate=pl.CostEstimate(flops=flops, bytes_accessed=2 << 20, transcendentals=1024 * 1152),
        name="attend",
    )(meta, q, own, far_k, far_v, rest, prev)


def cut_kernel(k_hbm, v_hbm, out, k, v, sems):
    pairs = ((k_hbm, k), (v_hbm, v))
    copies = [pltpu.make_async_copy(a, b, sems.at[i]) for i, (a, b) in enumerate(pairs)]
    for copy in copies:
        copy.start()
    for i, (_, x) in enumerate(pairs):
        copies[i].wait()
        for p in range(PIECES):
            rows = x[p * TILE : (p + 1) * TILE].astype(jnp.float32)
            out[i * PIECES + p] = jnp.swapaxes(rows, 0, 1).astype(out.dtype)


def cut(k, v):
    hbm = pl.BlockSpec(memory_space=pl.ANY)
    return pl.pallas_call(
        cut_kernel,
        out_shape=jax.ShapeDtypeStruct((2 * PIECES, 8, TILE, BS), k.dtype),
        in_specs=[hbm, hbm],
        out_specs=vmem(),
        scratch_shapes=[pltpu.VMEM(k.shape, k.dtype), pltpu.VMEM(v.shape, v.dtype), pltpu.SemaphoreType.DMA((2,))],
        compiler_params=pltpu.CompilerParams(vmem_limit_bytes=GRANT),
        name="cut",
    )(k, v)


def stage_kernel(q, out, sems):
    copies = [pltpu.make_async_copy(q.at[:, h * 8 : (h + 1) * 8], out.at[h], sems.at[h]) for h in range(8)]
    for copy in copies:
        copy.start()
    for copy in copies:
        copy.wait()


def stage(q):
    return pl.pallas_call(
        stage_kernel,
        out_shape=jax.ShapeDtypeStruct((8, BS, 8, BS), q.dtype),
        in_specs=[pl.BlockSpec(memory_space=pl.ANY)],
        out_specs=vmem(),
        scratch_shapes=[pltpu.SemaphoreType.DMA((8,))],
        compiler_params=pltpu.CompilerParams(vmem_limit_bytes=GRANT),
        name="stage",
    )(q)


def blank_kernel(out):
    pass


def blank(shape, dtype):
    return pl.pallas_call(
        blank_kernel,
        out_shape=jax.ShapeDtypeStruct(shape, dtype),
        out_specs=pl.BlockSpec(memory_space=pl.ANY),
        name="blank",
    )()


def local(n_head, queries, keys, values, ancestors, lengths):
    return attention(n_head, queries, keys, values, ancestors, lengths)


def attention(n_head, queries, keys, values, ancestors, lengths):
    n_seq = 32
    place, level = lax.axis_index("seq"), lax.axis_index("head")
    pool, rank = pool_of(ancestors)
    pools = pool[None]
    bit = 1
    while bit < n_seq:
        other = lax.ppermute(pools, "seq", [(i, i ^ bit) for i in range(n_seq)])
        pools = jnp.concatenate([pools, other], axis=0)
        bit *= 2

    named = lax.dynamic_slice_in_dim(ancestors, level, 1)
    ranks = lax.dynamic_slice_in_dim(rank, level, 1)
    far_len = jnp.take(lengths, named)
    own_len = lax.dynamic_slice_in_dim(lengths, place * n_head + level, 1)[None]
    count = (jnp.take(lengths, pool[:POOL]) + TILE - 1) // TILE
    slot = jnp.arange(POOL + 1, dtype=jnp.int32)
    offs = jnp.sum(jnp.where(slot[None, :POOL] < slot[:, None], count[None, :], 0), axis=1)
    over = offs[POOL] > ROOM
    far_off = jnp.sum(jnp.where(ranks.reshape(-1, 1) == slot[None, :POOL], offs[None, :POOL], 0), axis=1)[None]
    row = jnp.concatenate([far_off, far_len, own_len, over.astype(jnp.int32).reshape(1, 1)], axis=1)
    shifts = [0]
    for step in range(1, n_head // 2):
        shifts += [n_head - step, step]
    shifts.append(n_head // 2)
    heads = (level + jnp.array(shifts, jnp.int32)) % n_head
    meta = jnp.concatenate([heads[:, None], jnp.broadcast_to(row, (n_head, row.shape[1]))], axis=1)

    own = cut(keys, values)
    held = lax.all_to_all(own.reshape(n_seq * n_head, TILE, BS), ("seq", "head"), 0, 0, tiled=True)
    picked = pick(pools, place.astype(jnp.int32)[None], held)
    far = lax.all_to_all(picked, "seq", 0, 0, tiled=True)
    far_k, far_v, rest = pack(offs, far)
    shape = (n_head,) + rest.shape
    rest = lax.cond(
        over,
        lambda r: lax.all_to_all(jnp.broadcast_to(r[None], shape), "head", 0, 0, tiled=True),
        lambda r: blank(shape, r.dtype),
        rest,
    )

    up = [(i, (i + 1) % n_head) for i in range(n_head)]
    down = [(i, (i - 1) % n_head) for i in range(n_head)]
    out = blank(queries.shape, queries.dtype)
    queries = stage(queries)
    out = attend(0, meta, queries, own, far_k, far_v, rest, out)
    k_up = k_down = far_k
    v_up = v_down = far_v
    for step in range(1, n_head // 2 + 1):
        k_up = lax.ppermute(k_up, "head", up)
        v_down = lax.ppermute(v_down, "head", down)
        if step == n_head // 2:
            out = attend(n_head - 1, meta, queries, own, k_up, v_down, rest, out)
            break
        v_up = lax.ppermute(v_up, "head", up)
        k_down = lax.ppermute(k_down, "head", down)
        out = attend(2 * step - 1, meta, queries, own, k_up, v_up, rest, out)
        out = attend(2 * step, meta, queries, own, k_down, v_down, rest, out)
    return out


def solution(mesh):
    placed = (
        P(("seq", "head"), None, None),
        P(("seq", "head"), None, None),
        P(("seq", "head"), None, None),
        P("seq", None),
        P(),
    )
    body = functools.partial(local, mesh.shape["head"])
    return jax.shard_map(
        body, mesh=mesh, in_specs=placed, out_specs=P(("seq", "head"), None, None), check_vma=False
    )
```
